128 devices in a mesh: loop: 64 (over y, x, z_lo, core), rep: 2 (over z_hi).
Axes of the slice: x: 4, y: 4, z: 4 (z_hi: 2, z_lo: 2; z = z_hi * 2 + z_lo), core: 2. Of those that a mesh axis runs over, the one named last changes fastest.
Arguments:
- embeddings: bfloat16 [4096, 32, 1024], P('loop'), as said below
- lengths: int32 [4096], P('loop'), may hold values from 4 to 32
- candidate_ids: int32 [4096], P('loop'), may hold values from 0 to 255
Outputs:
- pair_scores: float32 [4096, 704], P('loop')
- consensus: float32 [4096], P('loop')
The draws below stay inside these ranges and needn't reach their ends.
Inputs may be any that keep to these rules, and one draw needn't show every extreme that they name: Token embeddings of each candidate step.
All inputs are finite; a program needn't handle non-finite values.
Results may differ from the reference program's by a relative error of at most 0.0043.
Values may be sent and summed in bfloat16 or wider, within the bound.
A program may use at most 384 MiB of HBM per device.

```python
import math
import jax
import jax.numpy as jnp
from jax import lax

EMBED_WIDTH = 1024
STEP_TOKENS = 32
STATES_DEV = 64
BLOCK_REACH = 5
ANSWERS = 256
STATES = 4096
N_LOOP = 64


def draw_embeddings(key, part):
    key_topic, key_pick, key_noise = jax.random.split(key, 3)
    topics = jax.random.normal(key_topic, (48, EMBED_WIDTH), jnp.float32)
    picked = jax.random.randint(key_pick, (STATES, STEP_TOKENS), 0, 48)
    themes = topics[picked]
    noise = jax.random.normal(key_noise, (STATES, STEP_TOKENS, EMBED_WIDTH), jnp.float32)
    values = themes + noise
    return values.astype(jnp.bfloat16)


def with_ends(drawn, own_key, least, high):
    place = [jax.random.randint(jax.random.fold_in(own_key, axis), (), 0, length) for axis, length in enumerate(drawn.shape)]
    longest = drawn.shape.index(max(drawn.shape))
    next_to = place[:longest] + [(place[longest] + 1) % drawn.shape[longest]] + place[longest + 1:]
    return drawn.at[tuple(place)].set(least).at[tuple(next_to)].set(high)


def setup_inputs(seed: int = 0) -> dict:
    keys = jax.random.split(jax.random.key(seed), 4)
    embeddings = draw_embeddings(jax.random.fold_in(keys[3], 71), 0)
    lengths = with_ends(jax.random.randint(keys[1], (STATES,), 4, STEP_TOKENS + 1), jax.random.fold_in(keys[1], 1), 4, STEP_TOKENS).astype(jnp.int32)
    candidate_ids = with_ends(jax.random.randint(keys[2], (STATES,), 0, ANSWERS), jax.random.fold_in(keys[2], 1), 0, ANSWERS - 1).astype(jnp.int32)
    return dict(embeddings=embeddings, lengths=lengths, candidate_ids=candidate_ids)


def token_scale(embeddings):
    values = embeddings.astype(jnp.float32)
    return lax.rsqrt(lax.optimization_barrier(jnp.mean(values * values, axis=-1)) + 1e-06) / math.sqrt(values.shape[-1])

def harmonic_scores(rows_emb, rows_len, cols_emb, cols_len):
    row_count, tokens, features = rows_emb.shape
    col_count = cols_emb.shape[0]
    row_scale = token_scale(rows_emb)
    col_scale = token_scale(cols_emb)
    similar = jnp.dot(rows_emb.reshape(row_count * tokens, features), cols_emb.reshape(col_count * tokens, features).T, preferred_element_type=jnp.float32)
    similar = similar.reshape(row_count, tokens, col_count, tokens)
    similar = similar * row_scale[:, :, None, None] * col_scale[None, None, :, :]
    position = jnp.arange(tokens, dtype=jnp.int32)
    row_valid = position[None, :] < rows_len[:, None]
    col_valid = position[None, :] < cols_len[:, None]
    best_col = lax.optimization_barrier(jnp.max(jnp.where(col_valid[None, None, :, :], similar, -4.0), axis=3))
    precision = lax.optimization_barrier(jnp.sum(jnp.where(row_valid[:, :, None], best_col, 0.0), axis=1)) / rows_len[:, None].astype(jnp.float32)
    best_row = lax.optimization_barrier(jnp.max(jnp.where(row_valid[:, :, None, None], similar, -4.0), axis=1))
    recall = lax.optimization_barrier(jnp.sum(jnp.where(col_valid[None, :, :], best_row, 0.0), axis=2)) / cols_len[None, :].astype(jnp.float32)
    return 2.0 * precision * recall / jnp.maximum(precision + recall, 0.5)

def reference(embeddings, lengths, candidate_ids):
    blocks = N_LOOP
    slots = 2 * BLOCK_REACH + 1
    emb_blocks = embeddings.reshape(blocks, STATES_DEV, STEP_TOKENS, EMBED_WIDTH)
    length_blocks = lengths.reshape(blocks, STATES_DEV)
    ident_blocks = candidate_ids.reshape(blocks, STATES_DEV)

    def one_block(index):
        rows_emb = lax.dynamic_index_in_dim(emb_blocks, index, 0, keepdims=False)
        rows_len = lax.dynamic_index_in_dim(length_blocks, index, 0, keepdims=False)
        results = []
        for distance in range(BLOCK_REACH + 1):
            other = ((index + distance) % blocks).astype(jnp.int32)
            results.append(harmonic_scores(rows_emb, rows_len, lax.dynamic_index_in_dim(emb_blocks, other, 0, keepdims=False), lax.dynamic_index_in_dim(length_blocks, other, 0, keepdims=False)))
        return jnp.stack(results)
    forward = lax.map(one_block, jnp.arange(blocks, dtype=jnp.int32))
    pieces = []
    for slot in range(slots):
        distance = slot - BLOCK_REACH
        if distance >= 0:
            pieces.append(forward[:, distance])
        else:
            pieces.append(jnp.swapaxes(jnp.roll(forward[:, -distance], -distance, axis=0), 1, 2))
    table = jnp.transpose(jnp.stack(pieces, axis=1), (0, 2, 1, 3))
    peers = jnp.stack([jnp.roll(ident_blocks, BLOCK_REACH - slot, axis=0) for slot in range(slots)], axis=1)
    same = ident_blocks[:, :, None, None] == peers[:, None, :, :]
    slot_index = jnp.arange(slots, dtype=jnp.int32)
    row_index = jnp.arange(STATES_DEV, dtype=jnp.int32)
    self_pair = (slot_index[None, :, None] == BLOCK_REACH) & (row_index[:, None, None] == row_index[None, None, :])
    keep = same & jnp.logical_not(self_pair)[None]
    consensus = lax.optimization_barrier(jnp.sum(jnp.where(keep, table, 0.0), axis=(2, 3))).reshape(STATES)
    return (table.reshape(STATES, slots * STATES_DEV), consensus)
```

```python
import jax, jax.numpy as jnp
from jax import lax
from jax.experimental import pallas as pl
from jax.experimental.pallas import tpu as pltpu
from jax.sharding import PartitionSpec as P

TOK = 32
HALF = 32
D = 1024
ROWS = TOK * HALF
GROUP = 16
CHUNK = 256


def prep_kernel(len_ref, meta_ref, emb_ref, out_ref, tmp):
    h, q = pl.program_id(0), pl.program_id(1)
    pos = lax.broadcasted_iota(jnp.int32, (TOK, 1), 0)

    def one(s, carry):
        x = emb_ref[s].astype(jnp.float32)
        ms = jnp.sum(x * x, axis=1, keepdims=True) * (1.0 / D)
        y = x * (lax.rsqrt(ms + 1e-06) * (1.0 / 32.0))
        n = len_ref[h * HALF + q * GROUP + s]
        y = jnp.where(pos < n, y, y[0:1, :])
        for k in range(D // 128):
            tmp[pl.ds(pl.multiple_of(k * GROUP * TOK + s * TOK, TOK), TOK), :] = y[:, k * 128:(k + 1) * 128]
        return carry

    lax.fori_loop(0, GROUP, one, 0, unroll=2)
    for t in range(TOK):
        for k in range(D // 128):
            rows = tmp[pl.ds(k * GROUP * TOK + t, GROUP, stride=TOK), :]
            out_ref[pl.ds(pl.multiple_of(t * HALF + q * GROUP, GROUP), GROUP), k * 128:(k + 1) * 128] = rows.astype(jnp.bfloat16)

    @pl.when(q == 0)
    def _():
        out_ref[ROWS:ROWS + 16, :] = meta_ref[...]


def prep(emb, lengths, meta):
    return pl.pallas_call(
        prep_kernel,
        grid=(2, HALF // GROUP),
        in_specs=[
            pl.BlockSpec(memory_space=pltpu.SMEM),
            pl.BlockSpec((None, 16, D), lambda h, q: (h, 0, 0)),
            pl.BlockSpec((GROUP, TOK, D), lambda h, q: (h * (HALF // GROUP) + q, 0, 0)),
        ],
        out_specs=pl.BlockSpec((None, ROWS + 16, D), lambda h, q: (h, 0, 0)),
        out_shape=jax.ShapeDtypeStruct((2, ROWS + 16, D), jnp.bfloat16),
        scratch_shapes=[pltpu.VMEM((GROUP * TOK * D // 128, 128), jnp.float32)],
    )(lengths, meta, emb)


def make_meta(lengths, ids):
    l = jnp.tile(lengths.reshape(2, 1, HALF), (1, 1, TOK)).astype(jnp.bfloat16)
    i = jnp.tile(ids.reshape(2, 1, HALF), (1, 1, TOK)).astype(jnp.bfloat16)
    return jnp.concatenate([l, i, jnp.zeros((2, 14, D), jnp.bfloat16)], axis=1)


def rows_of(x):
    return jnp.broadcast_to(x.astype(jnp.float32).reshape(2, HALF, 1), (2, HALF, 128))


OFFSETS = ((4, 5, -2, -1, 1), (4, 3, -2, -3, 1), (-4, -3, -2, -5, 1), (-4, -5, -2, 5, -3))


def taken_offsets(role):
    found = []
    for k in range(5):
        for other in range(4):
            if (other + OFFSETS[other][k]) % 4 == role:
                found.append(-OFFSETS[other][k])
    return found


def score_chunk(own_ref, vis_ref, best_ref, row_best_ref, n, first):
    for h in range(2):
        s = lax.dot_general(own_ref[h, 0:ROWS, :], vis_ref[n * CHUNK:(n + 1) * CHUNK, :],
                            (((1,), (1,)), ((), ())), preferred_element_type=jnp.float32)
        row_best_ref[h, :, n * CHUNK:(n + 1) * CHUNK] = jnp.max(s.reshape(TOK, HALF, CHUNK), axis=0)
        cb = s[:, 0:128]
        for k in range(1, CHUNK // 128):
            cb = jnp.maximum(cb, s[:, k * 128:(k + 1) * 128])
        best_ref[h] = cb if first else jnp.maximum(best_ref[h], cb)


def finish_scores(len_ref, id_ref, vis_ref, best_ref, row_best_ref, x_ref, t_ref):
    lane = lax.broadcasted_iota(jnp.int32, (1, 128), 1)
    extra = vis_ref[ROWS:ROWS + 16, :].astype(jnp.float32)
    col_len = extra[0:1, :]
    for h in range(2):
        row_len = len_ref[h]
        total = jnp.zeros((HALF, 128), jnp.float32)
        for t in range(TOK):
            b = best_ref[h, t * HALF:(t + 1) * HALF, :]
            b = jnp.maximum(b, pltpu.roll(b, 64, 1))
            b = jnp.maximum(b, pltpu.roll(b, 32, 1))
            total = total + jnp.where(row_len > float(t), b, 0.0)
        precision = total / row_len
        rec = jnp.zeros((HALF, 128), jnp.float32)
        for k in range(ROWS // 128):
            u = (lane // HALF + 4 * k).astype(jnp.float32)
            rec = rec + jnp.where(u < col_len[:, k * 128:(k + 1) * 128], row_best_ref[h, :, k * 128:(k + 1) * 128], 0.0)
        rec = rec + pltpu.roll(rec, 64, 1)
        rec = rec + pltpu.roll(rec, 32, 1)
        recall = rec / col_len[:, 0:128]
        x_ref[h * HALF:(h + 1) * HALF, :] = 2.0 * precision * recall / jnp.maximum(precision + recall, 0.5)
    x_ref[64:72, :] = jnp.broadcast_to(extra[1:2, 0:128], (8, 128))
    both = jnp.concatenate([x_ref[0:64, :], id_ref[...]], axis=0)
    t_ref[...] = both.T[0:HALF, :]


def assemble(role, id_ref, x_refs, t_refs, table_ref, sum_ref):
    lane = lax.broadcasted_iota(jnp.int32, (64, 128), 1)
    row = lax.broadcasted_iota(jnp.int32, (64, 128), 0)
    low = lane < 64
    first = (lane % 64) < 32
    ids = id_ref[...]

    def own(k):
        vals = jnp.where(first, x_refs[0](k)[0:64, :], x_refs[1](k)[0:64, :])
        theirs = jnp.where(first[0:8], x_refs[0](k)[64:72, :], x_refs[1](k)[64:72, :])
        return vals, jnp.concatenate([theirs] * 8, axis=0)

    def taken(k, upper):
        both = jnp.concatenate([t_refs[0](k)[...], t_refs[1](k)[...]], axis=0)
        turned = pltpu.roll(both, 64, 1)
        return (turned, both) if upper else (both, turned)

    for mine in range(4):
        @pl.when(role == mine)
        def _(mine=mine):
            taken_at = taken_offsets(mine)
            total = jnp.zeros((64, 128), jnp.float32)
            for p in range(6):
                parts = []
                for upper in range(2):
                    d = 2 * p + upper - 5
                    if d > 5:
                        parts.append(parts[0])
                        continue
                    if d == 0:
                        vals, theirs = own(0)
                        same = (theirs == ids) & ((lane % 64) != row)
                    else:
                        if d in OFFSETS[mine]:
                            vals, theirs = own(1 + OFFSETS[mine].index(d))
                        else:
                            vals, theirs = taken(1 + taken_at.index(d), upper)
                        same = theirs == ids
                    inside = (lane >= 64) if upper else low
                    total = total + jnp.where(same & inside, vals, 0.0)
                    parts.append(vals)
                tile = jnp.where(low, parts[0], parts[1])
                width = 128 if p < 5 else 64
                table_ref[:, p * 128:p * 128 + width] = tile[:, 0:width]
            sums = jnp.sum(total, axis=1, keepdims=True)
            sum_ref[...] = jnp.broadcast_to(sums, (64, 128)).T[0:1, :]


def score_kernel(len_ref, id_ref, own_ref, vis_ref, x_ref, t_ref, best, row_best):
    for n in range(ROWS // CHUNK):
        score_chunk(own_ref, vis_ref, best, row_best, n, n == 0)
    finish_scores(len_ref, id_ref, vis_ref, best, row_best, x_ref, t_ref)


def score(own, vis, len_rows, id_rows):
    return pl.pallas_call(
        score_kernel,
        in_specs=[pl.BlockSpec(memory_space=pltpu.VMEM)] * 4,
        out_specs=[pl.BlockSpec(memory_space=pltpu.VMEM)] * 2,
        out_shape=[jax.ShapeDtypeStruct((72, 128), jnp.float32), jax.ShapeDtypeStruct((HALF, 128), jnp.float32)],
        scratch_shapes=[pltpu.VMEM((2, ROWS, 128), jnp.float32), pltpu.VMEM((2, HALF, ROWS), jnp.float32)],
        cost_estimate=pl.CostEstimate(flops=4 * ROWS * ROWS * D, bytes_accessed=6 << 20, transcendentals=0),
        compiler_params=pltpu.CompilerParams(vmem_limit_bytes=32 << 20),
    )(len_rows, id_rows, own, vis)


def place_kernel(role_ref, id_ref, x0, t0, x1, t1, table_ref, sum_ref):
    x_refs = [lambda k, x=x: x[k] for x in (x0, x1)]
    t_refs = [lambda k, t=t: t[k - 1] for t in (t0, t1)]
    assemble(role_ref[0], id_ref, x_refs, t_refs, table_ref, sum_ref)


def place(role, id_rows, x0, t0, x1, t1):
    return pl.pallas_call(
        place_kernel,
        in_specs=[pl.BlockSpec(memory_space=pltpu.SMEM)] + [pl.BlockSpec(memory_space=pltpu.VMEM)] * 5,
        out_specs=[pl.BlockSpec(memory_space=pltpu.VMEM)] * 2,
        out_shape=[jax.ShapeDtypeStruct((64, 704), jnp.float32), jax.ShapeDtypeStruct((1, 64), jnp.float32)],
    )(role, id_rows, x0, t0, x1, t1)


def move(value, k, back=False):
    n = lax.axis_size("loop")
    pairs = [((b + OFFSETS[b % 4][k]) % n, b) for b in range(n)]
    if back:
        pairs = [(b, a) for a, b in pairs]
    return lax.ppermute(value, "loop", pairs)


def shards(embeddings, lengths, candidate_ids):
    rep = lax.axis_index("rep")
    role = (lax.axis_index("loop") % 4).astype(jnp.int32).reshape(1)
    own = prep(embeddings, lengths, make_meta(lengths, candidate_ids))
    mine = lax.dynamic_index_in_dim(own, rep, 0, keepdims=False)
    len_rows, id_rows = rows_of(lengths), rows_of(candidate_ids).reshape(64, 128)
    visitors = [mine] + [move(mine, k) for k in (4, 0, 1, 2, 3)]
    xs, ts = {}, {}
    for k, vis in zip((0, 5, 1, 2, 3, 4), visitors):
        xs[k], t = score(own, vis, len_rows, id_rows)
        if k:
            ts[k] = move(t, k - 1, back=True)
    x = jnp.stack([xs[k] for k in range(6)])
    t = jnp.stack([ts[k] for k in range(1, 6)])
    ox, ot = lax.ppermute((x, t), "rep", [(0, 1), (1, 0)])
    zero = rep == 0
    pick = lambda a, b: (jnp.where(zero, a, b), jnp.where(zero, b, a))
    (x0, x1), (t0, t1) = pick(x, ox), pick(t, ot)
    table, sums = place(role, id_rows, x0, t0, x1, t1)
    return table, sums.reshape(64)


def solution(mesh):
    placed = (P("loop", None, None), P("loop"), P("loop"))
    return jax.shard_map(
        shards, mesh=mesh, in_specs=placed, out_specs=(P("loop", None), P("loop")), check_vma=False
    )
```

```python
import jax, jax.numpy as jnp
from jax import lax
from jax.experimental import pallas as pl
from jax.experimental.pallas import tpu as pltpu
from jax.sharding import PartitionSpec as P

TOK = 32
HALF = 32
D = 1024
ROWS = TOK * HALF
GROUP = 16
CHUNK = 256
CHUNKS = ROWS // CHUNK
MESH = pl.DeviceIdType.MESH


def prep_kernel(len_ref, emb_ref, out_ref, tmp):
    h, q = pl.program_id(0), pl.program_id(1)
    pos = lax.broadcasted_iota(jnp.int32, (TOK, 1), 0)

    def one(s, carry):
        x = emb_ref[s].astype(jnp.float32)
        ms = jnp.sum(x * x, axis=1, keepdims=True) * (1.0 / D)
        y = x * (lax.rsqrt(ms + 1e-06) * (1.0 / 32.0))
        n = len_ref[h * HALF + q * GROUP + s]
        y = jnp.where(pos < n, y, y[0:1, :])
        for k in range(D // 128):
            tmp[pl.ds(pl.multiple_of(k * GROUP * TOK + s * TOK, TOK), TOK), :] = y[:, k * 128:(k + 1) * 128]
        return carry

    lax.fori_loop(0, GROUP, one, 0, unroll=2)
    for t in range(TOK):
        for k in range(D // 128):
            rows = tmp[pl.ds(k * GROUP * TOK + t, GROUP, stride=TOK), :]
            out_ref[t // 8, pl.ds(pl.multiple_of(t % 8 * HALF + q * GROUP, GROUP), GROUP), k * 128:(k + 1) * 128] = rows.astype(jnp.bfloat16)


def prep(emb, lengths):
    return pl.pallas_call(
        prep_kernel,
        grid=(2, HALF // GROUP),
        in_specs=[
            pl.BlockSpec(memory_space=pltpu.SMEM),
            pl.BlockSpec((GROUP, TOK, D), lambda h, q: (h * (HALF // GROUP) + q, 0, 0)),
        ],
        out_specs=pl.BlockSpec((None, CHUNKS, CHUNK, D), lambda h, q: (h, 0, 0, 0)),
        out_shape=jax.ShapeDtypeStruct((2, CHUNKS, CHUNK, D), jnp.bfloat16),
        scratch_shapes=[pltpu.VMEM((GROUP * TOK * D // 128, 128), jnp.float32)],
    )(lengths, emb)


def make_meta(lengths, ids):
    both = jnp.stack([lengths, ids]).astype(jnp.float32).reshape(2, 2, 1, HALF)
    both = jnp.tile(jnp.swapaxes(both, 0, 1), (1, 1, 4, 4)).reshape(2, 8, 128)
    return both


def rows_of(x):
    return jnp.broadcast_to(x.astype(jnp.float32).reshape(2, HALF, 1), (2, HALF, 128))


BLOCK_REACH = 5
OFFSETS = ((4, 5, -2, -1, 1), (4, 3, -2, -3, 1), (-4, -3, -2, -5, 1), (-4, -5, -2, 5, -3))


def taken_offsets(role):
    found = []
    for k in range(5):
        for other in range(4):
            if (other + OFFSETS[other][k]) % 4 == role:
                found.append(-OFFSETS[other][k])
    return found


def score_chunk(own_ref, cols, best_ref, row_best_ref, slot, n):
    for h in range(2):
        s = lax.dot_general(own_ref[h].reshape(ROWS, D), cols,
                            (((1,), (1,)), ((), ())), preferred_element_type=jnp.float32)
        row_best_ref[slot, h, n] = jnp.max(s.reshape(TOK, HALF, CHUNK), axis=0)
        cb = s[:, 0:128]
        for k in range(1, CHUNK // 128):
            cb = jnp.maximum(cb, s[:, k * 128:(k + 1) * 128])
        best_ref[slot, h] = jnp.maximum(best_ref[slot, h], cb)


def finish_scores(len_ref, id_ref, meta, best_ref, row_best_ref, slot, x_ref):
    lane = lax.broadcasted_iota(jnp.int32, (1, 128), 1)
    col_len = meta[0:1, :]
    for h in range(2):
        row_len = len_ref[h]
        total = jnp.zeros((HALF, 128), jnp.float32)
        for t in range(TOK):
            b = best_ref[slot, h, t * HALF:(t + 1) * HALF, :]
            b = jnp.maximum(b, pltpu.roll(b, 64, 1))
            b = jnp.maximum(b, pltpu.roll(b, 32, 1))
            total = total + jnp.where(row_len > float(t), b, 0.0)
        precision = total / row_len
        rec = jnp.zeros((HALF, 128), jnp.float32)
        for n in range(CHUNKS):
            for k in range(CHUNK // 128):
                u = (lane // HALF + 4 * (n * (CHUNK // 128) + k)).astype(jnp.float32)
                rec = rec + jnp.where(u < col_len, row_best_ref[slot, h, n, :, k * 128:(k + 1) * 128], 0.0)
        rec = rec + pltpu.roll(rec, 64, 1)
        rec = rec + pltpu.roll(rec, 32, 1)
        recall = rec / col_len
        x_ref[slot, h * HALF:(h + 1) * HALF, :] = 2.0 * precision * recall / jnp.maximum(precision + recall, 0.5)
    x_ref[slot, 64:72, :] = jnp.broadcast_to(meta[4:5, :], (8, 128))


def turn(x_ref, id_ref, slot, t_ref):
    both = jnp.concatenate([x_ref[slot, 0:64, :], id_ref[...]], axis=0)
    t_ref[slot] = both.T[0:HALF, :]


def main_kernel(len_ref, id_ref, meta_ref, own_ref, table_ref, sum_ref,
                vis, metas, best, row_best, x_mine, x_other, t_mine, t_got,
                send_sem, recv_sem, meta_send, meta_recv, x_send, x_recv, t_send, t_recv):
    n_loop = lax.axis_size("loop")
    b, r = lax.axis_index("loop"), lax.axis_index("rep")
    other = 1 - r
    role = b % 4
    is_a = role < 2
    early = 5 - 2 * (role // 2)
    late = 8 - early
    partner = b + 1 - 2 * (b % 2)

    def block(d):
        return (b + n_loop + d) % n_loop

    def copy(src, dst, ssem, rsem, blk, rp):
        return pltpu.make_async_remote_copy(src_ref=src, dst_ref=dst, send_sem=ssem, recv_sem=rsem,
                                            device_id={"loop": blk, "rep": rp}, device_id_type=MESH)

    barrier = pltpu.get_barrier_semaphore()
    peers = [(block(d), rp) for d in range(-BLOCK_REACH, BLOCK_REACH + 1) if d for rp in (r, other)]
    peers += [(b, other), (block(7), r), (block(-7), r)]
    for blk, rp in peers:
        pl.semaphore_signal(barrier, inc=1, device_id={"loop": blk, "rep": rp}, device_id_type=MESH)
    best[...] = jnp.full(best.shape, -4.0, jnp.float32)
    pl.semaphore_wait(barrier, len(peers))

    def move(kind, n, src, slot, blk, rp):
        return copy(src, vis.at[slot, n], send_sem.at[kind, n], recv_sem.at[slot, n], blk, rp)

    def arrived(slot, n):
        copy(vis.at[slot, n], vis.at[slot, n], send_sem.at[0, n], recv_sem.at[slot, n], partner, r).wait_recv()

    mine = own_ref.at[r]
    cross = own_ref.at[other]
    starts = {
        0: [(0, mine, 1, block(-4), r), (2, mine, 3, block(2), r)],
        1: [(4, mine, 5, block(-1), r), (0, mine, 1, block(-4), r), (5, mine, 0, block(4), r), (2, cross, 3, block(2), other)],
        2: [(0, mine, 1, block(4), r), (4, cross, 5, block(-1), other)],
        3: [(4, mine, 5, block(-1), r), (0, mine, 1, block(4), r)],
    }
    for me in range(4):
        @pl.when(role == me)
        def _(me=me):
            for n in range(CHUNKS):
                for kind, src, slot, blk, rp in starts[me]:
                    move(kind, n, src.at[n], slot, blk, rp).start()
            for k in range(5):
                d = taken_offsets(me)[k]
                copy(meta_ref.at[r], metas.at[k], meta_send.at[k], meta_recv.at[k], block(d), r).start()

    def after_early(n):
        return [(2, 7, vis.at[3, n], 5, block(1), r), (2, 3, vis.at[3, n], 4, block(-7), r)]

    def after_first(n):
        return [(0, 1, vis.at[1, n], 2, partner, r), (1, 1, vis.at[1, n], 2, partner, r),
                (2, 1, vis.at[1, n], 2, partner, r), (3, 1, vis.at[1, n], 2, partner, r),
                (2, 2, vis.at[1, n], 3, block(-2), r), (3, 2, vis.at[1, n], 3, block(-2), r)]

    def after_relay(n):
        return [(1, 6, vis.at[0, n], 4, block(1), r)]

    def after_late(n):
        return [(0, 3, vis.at[3, n], 4, partner, r), (1, 3, vis.at[3, n], 4, partner, r)]

    def forward(list_of, n):
        for me in range(4):
            todo = [x for x in list_of(n) if x[0] == me]
            if todo:
                @pl.when(role == me)
                def _(todo=todo):
                    for _, kind, src, slot, blk, rp in todo:
                        move(kind, n, src, slot, blk, rp).start()

    def compute(slot, n):
        score_chunk(own_ref, vis[slot, n], best, row_best, slot, n)

    def second_part(n):
        arrived(late, n)
        forward(after_late, n)
        compute(late, n)
        arrived(4, n)
        compute(4, n)

    def self_step(n, carry):
        score_chunk(own_ref, own_ref[r, n], best, row_best, 0, n)
        return carry

    lax.fori_loop(0, CHUNKS, self_step, 0)

    def step(n, carry):
        arrived(early, n)
        forward(after_early, n)
        compute(early, n)
        arrived(1, n)
        forward(after_first, n)
        compute(1, n)

        @pl.when(role == 1)
        def _():
            arrived(0, n)
            forward(after_relay, n)

        arrived(2, n)
        compute(2, n)

        @pl.when(n > 0)
        def _():
            second_part(n - 1)
        return carry

    lax.fori_loop(0, CHUNKS, step, 0)

    for k in range(5):
        copy(metas.at[k], metas.at[k], meta_send.at[k], meta_recv.at[k], partner, r).wait_recv()

    def results(slot, me):
        blk = block(OFFSETS[me][slot - 1])
        out = [copy(x_mine.at[slot], x_other.at[slot], x_send.at[slot], x_recv.at[slot], b, other)]
        for i, rp in enumerate((r, other)):
            out.append(copy(t_mine.at[slot], t_got.at[r, slot], t_send.at[i, slot], t_recv.at[r, slot], blk, rp))
        return out

    def finish(slot, meta):
        finish_scores(len_ref, id_ref, meta, best, row_best, slot, x_mine)

    finish(0, meta_ref[r])
    for slot in (early, 1, 2):
        finish(slot, metas[slot - 1])
        turn(x_mine, id_ref, slot, t_mine)
    second_part(CHUNKS - 1)
    own_result = copy(x_mine.at[0], x_other.at[0], x_send.at[0], x_recv.at[0], b, other)
    own_result.start()
    for me in range(4):
        @pl.when(role == me)
        def _(me=me):
            for slot in (5 if me < 2 else 3, 1, 2):
                for c in results(slot, me):
                    c.start()
    for slot in (late, 4):
        finish(slot, metas[slot - 1])
        turn(x_mine, id_ref, slot, t_mine)
    for me in range(4):
        @pl.when(role == me)
        def _(me=me):
            for slot in (3 if me < 2 else 5, 4):
                for c in results(slot, me):
                    c.start()
    for slot in range(6):
        copy(x_mine.at[slot], x_other.at[slot], x_send.at[slot], x_recv.at[slot], b, other).wait_recv()
    for slot in range(1, 6):
        for i in range(2):
            copy(t_mine.at[slot], t_got.at[i, slot], t_send.at[i, slot], t_recv.at[i, slot], b, other).wait_recv()

    xs = [lambda k: _Pick(r == 0, x_mine.at[k], x_other.at[k]), lambda k: _Pick(r == 0, x_other.at[k], x_mine.at[k])]
    ts = [lambda k: t_got.at[0, k], lambda k: t_got.at[1, k]]
    assemble(role, id_ref, xs, ts, table_ref, sum_ref)

    own_result.wait_send()
    for me in range(4):
        @pl.when(role == me)
        def _(me=me):
            for n in range(CHUNKS):
                for kind, src, slot, blk, rp in starts[me]:
                    move(kind, n, src.at[n], slot, blk, rp).wait_send()
                for list_of in (after_early, after_first, after_relay, after_late):
                    for who, kind, src, slot, blk, rp in list_of(n):
                        if who == me:
                            move(kind, n, src, slot, blk, rp).wait_send()
            for k in range(5):
                d = taken_offsets(me)[k]
                copy(meta_ref.at[r], metas.at[k], meta_send.at[k], meta_recv.at[k], block(d), r).wait_send()
            for slot in range(1, 6):
                for c in results(slot, me):
                    c.wait_send()


class _Pick:
    def __init__(self, take, one, two):
        self.take, self.one, self.two = take, one, two

    def __getitem__(self, at):
        return jnp.where(self.take, self.one[at], self.two[at])


def assemble(role, id_ref, x_refs, t_refs, table_ref, sum_ref):
    lane = lax.broadcasted_iota(jnp.int32, (64, 128), 1)
    row = lax.broadcasted_iota(jnp.int32, (64, 128), 0)
    low = lane < 64
    first = (lane % 64) < 32
    ids = id_ref[...]

    def own(k):
        vals = jnp.where(first, x_refs[0](k)[0:64, :], x_refs[1](k)[0:64, :])
        theirs = jnp.where(first[0:8], x_refs[0](k)[64:72, :], x_refs[1](k)[64:72, :])
        return vals, jnp.concatenate([theirs] * 8, axis=0)

    def taken(k, upper):
        both = jnp.concatenate([t_refs[0](k)[...], t_refs[1](k)[...]], axis=0)
        turned = pltpu.roll(both, 64, 1)
        return (turned, both) if upper else (both, turned)

    for mine in range(4):
        @pl.when(role == mine)
        def _(mine=mine):
            taken_at = taken_offsets(mine)
            total = jnp.zeros((64, 128), jnp.float32)
            for p in range(6):
                parts = []
                for upper in range(2):
                    d = 2 * p + upper - 5
                    if d > 5:
                        parts.append(parts[0])
                        continue
                    if d == 0:
                        vals, theirs = own(0)
                        same = (theirs == ids) & ((lane % 64) != row)
                    else:
                        if d in OFFSETS[mine]:
                            vals, theirs = own(1 + OFFSETS[mine].index(d))
                        else:
                            vals, theirs = taken(1 + taken_at.index(d), upper)
                        same = theirs == ids
                    inside = (lane >= 64) if upper else low
                    total = total + jnp.where(same & inside, vals, 0.0)
                    parts.append(vals)
                tile = jnp.where(low, parts[0], parts[1])
                width = 128 if p < 5 else 64
                table_ref[:, p * 128:p * 128 + width] = tile[:, 0:width]
            sums = jnp.sum(total, axis=1, keepdims=True)
            sum_ref[...] = jnp.broadcast_to(sums, (64, 128)).T[0:1, :]


def shards(embeddings, lengths, candidate_ids):
    own = prep(embeddings, lengths)
    vmem, dma = pltpu.VMEM, pltpu.SemaphoreType.DMA
    f32 = jnp.float32
    table, sums = pl.pallas_call(
        main_kernel,
        in_specs=[pl.BlockSpec(memory_space=pltpu.VMEM)] * 4,
        out_specs=[pl.BlockSpec(memory_space=pltpu.VMEM)] * 2,
        out_shape=[jax.ShapeDtypeStruct((64, 704), f32), jax.ShapeDtypeStruct((1, 64), f32)],
        scratch_shapes=[
            vmem((6, CHUNKS, CHUNK, D), jnp.bfloat16),
            vmem((5, 8, 128), f32),
            vmem((6, 2, ROWS, 128), f32),
            vmem((6, 2, CHUNKS, HALF, CHUNK), f32),
            vmem((6, 72, 128), f32),
            vmem((6, 72, 128), f32),
            vmem((6, HALF, 128), f32),
            vmem((2, 6, HALF, 128), f32),
            dma((8, CHUNKS)),
            dma((6, CHUNKS)),
            dma((5,)),
            dma((5,)),
            dma((6,)),
            dma((6,)),
            dma((2, 6)),
            dma((2, 6)),
        ],
        compiler_params=pltpu.CompilerParams(collective_id=0, has_side_effects=True, vmem_limit_bytes=56 << 20),
    )(rows_of(lengths), rows_of(candidate_ids).reshape(64, 128), make_meta(lengths, candidate_ids), own)
    return table, sums.reshape(64)


def solution(mesh):
    placed = (P("loop", None, None), P("loop"), P("loop"))
    return jax.shard_map(
        shards, mesh=mesh, in_specs=placed, out_specs=(P("loop", None), P("loop")), check_vma=False
    )
```

```python
import jax
import jax.numpy as jnp
from jax import lax
from jax.experimental import pallas as pl
from jax.experimental.pallas import tpu as pltpu
from jax.sharding import PartitionSpec as P

BLOCK_REACH = 5
TOK = 32
HALF = 32
D = 1024
ROWS = TOK * HALF
GROUP = 16
CHUNK = 256
CHUNKS = ROWS // CHUNK
PIECE = 128
PIECES = ROWS // PIECE
MESH = pl.DeviceIdType.MESH
OFFSETS = ((4, 5, -2, -1, 1), (4, 3, -2, -3, 1), (-4, -3, -2, -5, 1), (-4, -5, -2, 5, -3))


def taken_offsets(role):
    found = []
    for k in range(5):
        for other in range(4):
            if (other + OFFSETS[other][k]) % 4 == role:
                found.append(-OFFSETS[other][k])
    return found


def prep_kernel(len_ref, lens_ref, ids_ref, emb_ref, out_ref, len_rows_ref, id_rows_ref, meta_ref, tmp):
    h, q = pl.program_id(0), pl.program_id(1)
    pos = lax.broadcasted_iota(jnp.int32, (TOK, 1), 0)

    def one(s, carry):
        x = emb_ref[s].astype(jnp.float32)
        ms = jnp.sum(x * x, axis=1, keepdims=True) * (1.0 / D)
        y = x * (lax.rsqrt(ms + 1e-06) * (1.0 / 32.0))
        n = len_ref[h * HALF + q * GROUP + s]
        y = jnp.where(pos < n, y, y[0:1, :])
        for k in range(D // 128):
            tmp[pl.ds(pl.multiple_of(k * GROUP * TOK + s * TOK, TOK), TOK), :] = y[:, k * 128:(k + 1) * 128]
        return carry

    lax.fori_loop(0, GROUP, one, 0, unroll=4)
    for t in range(TOK):
        row = pl.multiple_of(t % 4 * HALF + q * GROUP, GROUP)
        for k in range(D // 128):
            rows = tmp[pl.ds(k * GROUP * TOK + t, GROUP, stride=TOK), :]
            out_ref[t // 4, pl.ds(row, GROUP), k * 128:(k + 1) * 128] = rows.astype(jnp.bfloat16)

    @pl.when((h == 0) & (q == 0))
    def _():
        lane = lax.broadcasted_iota(jnp.int32, (1, 128), 1)
        even = lane // HALF % 2 == 0
        for ref, rows_ref, at in ((lens_ref, len_rows_ref, 0), (ids_ref, id_rows_ref, 4)):
            line = ref[...].astype(jnp.float32)
            rows_ref[...] = jnp.broadcast_to(line, (128, 64)).T
            twice = jnp.concatenate([line, line], axis=1)
            turned = pltpu.roll(twice, HALF, 1)
            meta_ref[0, at:at + 4, :] = jnp.broadcast_to(jnp.where(even, twice, turned), (4, 128))
            meta_ref[1, at:at + 4, :] = jnp.broadcast_to(jnp.where(even, turned, twice), (4, 128))


def prep(emb, lengths, ids):
    whole = lambda shape: pl.BlockSpec(shape, lambda h, q: (0,) * len(shape))
    f32 = jnp.float32
    return pl.pallas_call(
        prep_kernel,
        grid=(2, HALF // GROUP),
        in_specs=[
            pl.BlockSpec(memory_space=pltpu.SMEM),
            whole((1, 64)),
            whole((1, 64)),
            pl.BlockSpec((GROUP, TOK, D), lambda h, q: (h * (HALF // GROUP) + q, 0, 0)),
        ],
        out_specs=[pl.BlockSpec((None, PIECES, PIECE, D), lambda h, q: (h, 0, 0, 0)),
                   whole((64, 128)), whole((64, 128)), whole((2, 8, 128))],
        out_shape=[jax.ShapeDtypeStruct((2, PIECES, PIECE, D), jnp.bfloat16), jax.ShapeDtypeStruct((64, 128), f32),
                   jax.ShapeDtypeStruct((64, 128), f32), jax.ShapeDtypeStruct((2, 8, 128), f32)],
        scratch_shapes=[pltpu.VMEM((GROUP * TOK * D // 128, 128), f32)],
    )(lengths, lengths.reshape(1, 64), ids.reshape(1, 64), emb)


def score_chunk(own_ref, cols, best_ref, row_best_ref, slot, n):
    for h in range(2):
        s = lax.dot_general(own_ref[h].reshape(ROWS, D), cols,
                            (((1,), (1,)), ((), ())), preferred_element_type=jnp.float32)
        row_best_ref[slot, h, n] = jnp.max(s.reshape(TOK, HALF, CHUNK), axis=0)
        cb = s[:, 0:128]
        for k in range(1, CHUNK // 128):
            cb = jnp.maximum(cb, s[:, k * 128:(k + 1) * 128])
        best_ref[slot, h] = jnp.maximum(best_ref[slot, h], cb)


def finish_scores(len_ref, id_ref, meta, best_ref, row_best_ref, slot, x_ref, t_ref):
    lane = lax.broadcasted_iota(jnp.int32, (1, 128), 1)
    col_len = meta[0:1, :]
    scores = []
    for h in range(2):
        row_len = len_ref[h * HALF:(h + 1) * HALF, :]

        def add(t, total):
            b = best_ref[slot, h, pl.ds(pl.multiple_of(t * HALF, HALF), HALF), :]
            b = jnp.maximum(b, pltpu.roll(b, 64, 1))
            b = jnp.maximum(b, pltpu.roll(b, 32, 1))
            return total + jnp.where(row_len > t.astype(jnp.float32), b, 0.0)

        precision = lax.fori_loop(0, TOK, add, jnp.zeros((HALF, 128), jnp.float32), unroll=8) / row_len
        rec = jnp.zeros((HALF, 128), jnp.float32)
        for n in range(CHUNKS):
            for k in range(CHUNK // 128):
                u = (lane // HALF + 4 * (n * (CHUNK // 128) + k)).astype(jnp.float32)
                rec = rec + jnp.where(u < col_len, row_best_ref[slot, h, n, :, k * 128:(k + 1) * 128], 0.0)
        rec = rec + pltpu.roll(rec, 64, 1)
        rec = rec + pltpu.roll(rec, 32, 1)
        recall = rec / col_len
        score = 2.0 * precision * recall / jnp.maximum(precision + recall, 0.5)
        x_ref[slot, h * HALF:(h + 1) * HALF, :] = score
        scores.append(score)
    x_ref[slot, 64:72, :] = jnp.broadcast_to(meta[4:5, :], (8, 128))
    t_ref[slot] = jnp.concatenate(scores + [id_ref[...]], axis=0).T[0:HALF, :]


def main_kernel(len_ref, id_ref, meta_ref, own_ref, x_out, t_out,
                vis, metas, best, row_best, x_mine, x_other, t_mine, t_got,
                send_sem, recv_sem, self_sem, meta_send, meta_recv, x_send, x_recv, t_send, t_recv):
    n_loop = lax.axis_size("loop")
    b, r = lax.axis_index("loop"), lax.axis_index("rep")
    other = 1 - r
    role = b % 4
    half, core = role // 2, role % 2
    early = 5 - 2 * half
    late = 8 - early
    partner = b + 1 - 2 * core

    def block(d):
        return (b + n_loop + d) % n_loop

    def by_role(values):
        v = values
        return v[0] * (1 - half) * (1 - core) + v[1] * (1 - half) * core + v[2] * half * (1 - core) + v[3] * half * core

    def copy(src, dst, ssem, rsem, blk, rp):
        return pltpu.make_async_remote_copy(src_ref=src, dst_ref=dst, send_sem=ssem, recv_sem=rsem,
                                            device_id={"loop": blk, "rep": rp}, device_id_type=MESH)

    barrier = pltpu.get_barrier_semaphore()
    peers = [(block(d), rp) for d in range(-BLOCK_REACH, BLOCK_REACH + 1) if d for rp in (r, other)]
    peers += [(b, other)]
    for blk, rp in peers:
        pl.semaphore_signal(barrier, inc=1, device_id={"loop": blk, "rep": rp}, device_id_type=MESH)
    to_self = pltpu.make_async_copy(own_ref.at[r], vis.at[6], self_sem)
    to_self.start()
    metas[0] = meta_ref[r]

    def clear(i, carry):
        best[i // 2, i % 2] = jnp.full((ROWS, 128), -4.0, jnp.float32)
        return carry

    lax.fori_loop(0, 12, clear, 0)
    pl.semaphore_wait(barrier, len(peers))

    def move(kind, f, src, slot, blk, rp):
        return copy(src, vis.at[slot, f], send_sem.at[kind, f], recv_sem.at[slot, f], blk, rp)

    def arrived(slot, f):
        copy(vis.at[slot, f], vis.at[slot, f], send_sem.at[0, f], recv_sem.at[slot, f], partner, r).wait_recv()

    mine = own_ref.at[r]
    cross = own_ref.at[other]
    starts = {
        0: [(0, mine, 1, block(-4), r), (2, mine, 3, block(2), r)],
        1: [(0, mine, 1, block(-4), r), (4, mine, 5, block(-1), r), (5, mine, 0, block(4), r), (2, cross, 3, block(2), other)],
        2: [(0, mine, 1, block(4), r), (4, cross, 5, block(-1), other)],
        3: [(0, mine, 1, block(4), r), (4, mine, 5, block(-1), r)],
    }

    def first_moves(me, then):
        def one(f, carry):
            for kind, src, slot, blk, rp in starts[me]:
                then(move(kind, f, src.at[f], slot, blk, rp))
            return carry

        lax.fori_loop(0, PIECES, one, 0)

    for me in range(4):
        @pl.when(role == me)
        def _(me=me):
            first_moves(me, lambda c: c.start())

    def meta_copy(k):
        blk = block(by_role([taken_offsets(me)[k] for me in range(4)]))
        return copy(meta_ref.at[r], metas.at[k + 1], meta_send.at[k], meta_recv.at[k], blk, r)

    for k in range(5):
        meta_copy(k).start()

    def after_early(f):
        return [(2, 7, vis.at[3, f], 5, block(1), r), (2, 3, vis.at[3, f], 0, block(-3), r)]

    def after_first(f):
        return [(0, 1, vis.at[1, f], 2, partner, r), (1, 1, vis.at[1, f], 2, partner, r),
                (2, 1, vis.at[1, f], 2, partner, r), (3, 1, vis.at[1, f], 2, partner, r),
                (2, 2, vis.at[1, f], 3, block(-2), r), (3, 2, vis.at[1, f], 3, block(-2), r)]

    def after_relay(f):
        return [(1, 6, vis.at[0, f], 4, block(1), r), (3, 6, vis.at[0, f], 4, block(-4), r)]

    def after_late(f):
        return [(0, 3, vis.at[3, f], 4, partner, r), (1, 3, vis.at[3, f], 4, partner, r)]

    def forward(list_of, f):
        for me in range(4):
            todo = [x for x in list_of(f) if x[0] == me]
            if todo:
                @pl.when(role == me)
                def _(todo=todo):
                    for _, kind, src, slot, blk, rp in todo:
                        move(kind, f, src, slot, blk, rp).start()

    def results(slot):
        out = [copy(x_mine.at[slot], x_other.at[slot], x_send.at[slot], x_recv.at[slot], b, other)]
        if slot:
            blk = block(by_role([OFFSETS[me][slot - 1] for me in range(4)]))
            for i, rp in enumerate((r, other)):
                out.append(copy(t_mine.at[slot], t_got.at[r, slot], t_send.at[i, slot], t_recv.at[r, slot], blk, rp))
        return out

    def send_results(slot):
        for c in results(slot):
            c.start()

    def send_either(one, two):
        pl.when(half == 0)(lambda: send_results(one))
        pl.when(half == 1)(lambda: send_results(two))

    def step(f, carry):
        odd = f % 2

        @pl.when(f < PIECES)
        def _():
            arrived(early, f)
            forward(after_early, f)
            arrived(1, f)
            forward(after_first, f)

            @pl.when(core == 1)
            def _():
                arrived(0, f)
                forward(after_relay, f)

        @pl.when(f > 0)
        def _():
            arrived(late, f - 1)
            forward(after_late, f - 1)

        @pl.when(f == PIECES - 1)
        def _():
            for k in range(5):
                copy(metas.at[k + 1], metas.at[k + 1], meta_send.at[k], meta_recv.at[k], partner, r).wait_recv()

        def part(i, carry):
            slot = odd * (early * (1 - i) + i) + (1 - odd) * ((1 - i) * (2 - i) + late * i * (2 - i) + 2 * i * (i - 1))
            n = (f - 1) // 2

            @pl.when((1 - odd) * (i - 1) != 0)
            def _():
                arrived(slot, 2 * n)
                arrived(slot, 2 * n + 1)

            @pl.when((f == PIECES) & (i == 0))
            def _():
                send_results(0)
                send_either(5, 3)
                send_results(1)

            @pl.when((f == PIECES) & (i == 1))
            def _():
                send_results(2)

            @pl.when((f == PIECES) & (i == 2))
            def _():
                send_either(3, 5)

            scored(slot, slot, n)
            return carry

        @pl.when(f > 0)
        def _():
            lax.fori_loop(0, 3 - odd, part, 0)
        return carry

    def scored(slot, source, n):
        cols = vis[source, pl.ds(2 * n, 2)].reshape(CHUNK, D)
        score_chunk(own_ref, cols, best, row_best, slot, n)

        @pl.when(n == CHUNKS - 1)
        def _():
            finish_scores(len_ref, id_ref, metas[slot], best, row_best, slot, x_mine, t_mine)

    to_self.wait()

    def self_step(n, carry):
        scored(0, 6, n)
        return carry

    lax.fori_loop(0, CHUNKS, self_step, 0)
    lax.fori_loop(0, PIECES + 1, step, 0)

    for slot in range(6):
        x_out[r, slot] = x_mine[slot]
    send_results(4)
    for slot in range(6):
        copy(x_mine.at[slot], x_other.at[slot], x_send.at[slot], x_recv.at[slot], b, other).wait_recv()
        x_out[other, slot] = x_other[slot]
    for slot in range(1, 6):
        for i in range(2):
            copy(t_mine.at[slot], t_got.at[i, slot], t_send.at[i, slot], t_recv.at[i, slot], b, other).wait_recv()
            t_out[i, slot - 1] = t_got[i, slot]

    for slot in range(6):
        for c in results(slot):
            c.wait_send()
    for k in range(5):
        meta_copy(k).wait_send()
    for me in range(4):
        @pl.when(role == me)
        def _(me=me):
            first_moves(me, lambda c: c.wait_send())

            def rest(f, carry):
                for list_of in (after_early, after_first, after_relay, after_late):
                    for who, kind, src, slot, blk, rp in list_of(f):
                        if who == me:
                            move(kind, f, src, slot, blk, rp).wait_send()
                return carry

            lax.fori_loop(0, PIECES, rest, 0)


def place_kernel(role_ref, id_ref, x_ref, t_ref, table_ref, sum_ref):
    role = role_ref[0]
    lane = lax.broadcasted_iota(jnp.int32, (64, 128), 1)
    row = lax.broadcasted_iota(jnp.int32, (64, 128), 0)
    low = lane < 64
    first = (lane % 64) < 32
    ids = id_ref[...]

    def own(k):
        vals = jnp.where(first, x_ref[0, k, 0:64, :], x_ref[1, k, 0:64, :])
        theirs = jnp.where(first[0:8], x_ref[0, k, 64:72, :], x_ref[1, k, 64:72, :])
        return vals, jnp.concatenate([theirs] * 8, axis=0)

    def taken(k, upper):
        both = jnp.concatenate([t_ref[0, k], t_ref[1, k]], axis=0)
        turned = pltpu.roll(both, 64, 1)
        return (turned, both) if upper else (both, turned)

    for mine in range(4):
        @pl.when(role == mine)
        def _(mine=mine):
            taken_at = taken_offsets(mine)
            total = jnp.zeros((64, 128), jnp.float32)
            for p in range(6):
                parts = []
                for upper in range(2):
                    d = 2 * p + upper - BLOCK_REACH
                    if d > BLOCK_REACH:
                        parts.append(parts[0])
                        continue
                    if d == 0:
                        vals, theirs = own(0)
                        same = (theirs == ids) & ((lane % 64) != row)
                    else:
                        if d in OFFSETS[mine]:
                            vals, theirs = own(1 + OFFSETS[mine].index(d))
                        else:
                            vals, theirs = taken(taken_at.index(d), upper)
                        same = theirs == ids
                    inside = (lane >= 64) if upper else low
                    total = total + jnp.where(same & inside, vals, 0.0)
                    parts.append(vals)
                tile = jnp.where(low, parts[0], parts[1])
                width = 128 if p < 5 else 64
                table_ref[:, p * 128:p * 128 + width] = tile[:, 0:width]
            sums = jnp.sum(total, axis=1, keepdims=True)
            sum_ref[...] = jnp.broadcast_to(sums, (64, 128)).T[0:1, :]


def shards(embeddings, lengths, candidate_ids):
    own, len_rows, id_rows, meta = prep(embeddings, lengths, candidate_ids)
    vmem, dma, f32 = pltpu.VMEM, pltpu.SemaphoreType.DMA, jnp.float32
    in_vmem = pl.BlockSpec(memory_space=pltpu.VMEM)
    x, t = pl.pallas_call(
        main_kernel,
        in_specs=[in_vmem] * 4,
        out_specs=[in_vmem] * 2,
        out_shape=[jax.ShapeDtypeStruct((2, 6, 72, 128), f32), jax.ShapeDtypeStruct((2, 5, HALF, 128), f32)],
        scratch_shapes=[
            vmem((7, PIECES, PIECE, D), jnp.bfloat16),
            vmem((6, 8, 128), f32),
            vmem((6, 2, ROWS, 128), f32),
            vmem((6, 2, CHUNKS, HALF, CHUNK), f32),
            vmem((6, 72, 128), f32),
            vmem((6, 72, 128), f32),
            vmem((6, HALF, 128), f32),
            vmem((2, 6, HALF, 128), f32),
            dma((8, PIECES)),
            dma((6, PIECES)),
            dma,
            dma((5,)),
            dma((5,)),
            dma((6,)),
            dma((6,)),
            dma((2, 6)),
            dma((2, 6)),
        ],
        compiler_params=pltpu.CompilerParams(collective_id=0, has_side_effects=True, vmem_limit_bytes=56 << 20),
    )(len_rows, id_rows, meta, own)
    role = (lax.axis_index("loop") % 4).astype(jnp.int32).reshape(1)
    table, sums = pl.pallas_call(
        place_kernel,
        in_specs=[pl.BlockSpec(memory_space=pltpu.SMEM)] + [in_vmem] * 3,
        out_specs=[in_vmem] * 2,
        out_shape=[jax.ShapeDtypeStruct((64, 704), f32), jax.ShapeDtypeStruct((1, 64), f32)],
    )(role, id_rows, x, t)
    return table, sums.reshape(64)


def solution(mesh):
    placed = (P("loop", None, None), P("loop"), P("loop"))
    return jax.shard_map(
        shards, mesh=mesh, in_specs=placed, out_specs=(P("loop", None), P("loop")), check_vma=False
    )
```

```python
import jax
import jax.numpy as jnp
from jax import lax
from jax.experimental import pallas as pl
from jax.experimental.pallas import tpu as pltpu
from jax.sharding import PartitionSpec as P

BLOCK_REACH = 5
TOK = 32
HALF = 32
D = 1024
ROWS = TOK * HALF
GROUP = 16
CHUNK = 256
CHUNKS = ROWS // CHUNK
PIECES = 8
MESH = pl.DeviceIdType.MESH
OFFSETS = ((4, 5, -2, -1, 1), (4, 3, -2, -3, 1), (-4, -3, -2, -5, 1), (-4, -5, -2, 5, -3))


def taken_offsets(role):
    found = []
    for k in range(5):
        for other in range(4):
            if (other + OFFSETS[other][k]) % 4 == role:
                found.append(-OFFSETS[other][k])
    return found


def rows_of(line):
    return jnp.broadcast_to(line.astype(jnp.float32), (128, 64)).T


def turned_tokens():
    out = lax.broadcasted_iota(jnp.int32, (256, 256), 0)
    into = lax.broadcasted_iota(jnp.int32, (256, 256), 1)
    hit = (out // 16 == into % 16) & (out % 16 == into // 16)
    return jnp.where(hit, 1.0, 0.0).astype(jnp.bfloat16)


def prepare(emb, turn, lens, put):
    first = None
    for g in range(TOK // 16):
        raw = emb[:, g * 16:(g + 1) * 16, :].reshape(256, D)
        x = jnp.dot(turn, raw, preferred_element_type=jnp.float32)
        for t in range(16):
            rows = x[t * GROUP:(t + 1) * GROUP, :]
            ms = jnp.sum(rows * rows, axis=1, keepdims=True) * (1.0 / D)
            rows = rows * (lax.rsqrt(ms + 1e-06) * (1.0 / 32.0))
            if first is None:
                first = rows
            else:
                rows = jnp.where(lens > float(g * 16 + t), rows, first)
            put(g * 16 + t, rows.astype(jnp.bfloat16))


def score_chunk(own_ref, cols, best_ref, row_best_ref, slot, n):
    for h in range(2):
        s = lax.dot_general(own_ref[h].reshape(ROWS, D), cols,
                            (((1,), (1,)), ((), ())), preferred_element_type=jnp.float32)
        row_best_ref[slot, h, n] = jnp.max(s.reshape(TOK, HALF, CHUNK), axis=0)
        cb = s[:, 0:128]
        for k in range(1, CHUNK // 128):
            cb = jnp.maximum(cb, s[:, k * 128:(k + 1) * 128])
        best_ref[slot, h] = jnp.maximum(best_ref[slot, h], cb)


def finish_scores(len_ref, id_ref, meta, best_ref, row_best_ref, slot, x_ref, t_ref):
    lane = lax.broadcasted_iota(jnp.int32, (1, 128), 1)
    col_len = meta[0:1, :]
    scores = []
    for h in range(2):
        row_len = len_ref[h * HALF:(h + 1) * HALF, :]

        def add(t, total):
            b = best_ref[slot, h, pl.ds(pl.multiple_of(t * HALF, HALF), HALF), :]
            b = jnp.maximum(b, pltpu.roll(b, 64, 1))
            b = jnp.maximum(b, pltpu.roll(b, 32, 1))
            return total + jnp.where(row_len > t.astype(jnp.float32), b, 0.0)

        precision = lax.fori_loop(0, TOK, add, jnp.zeros((HALF, 128), jnp.float32), unroll=8) / row_len
        rec = jnp.zeros((HALF, 128), jnp.float32)
        for n in range(CHUNKS):
            for k in range(CHUNK // 128):
                u = (lane // HALF + 4 * (n * (CHUNK // 128) + k)).astype(jnp.float32)
                rec = rec + jnp.where(u < col_len, row_best_ref[slot, h, n, :, k * 128:(k + 1) * 128], 0.0)
        rec = rec + pltpu.roll(rec, 64, 1)
        rec = rec + pltpu.roll(rec, 32, 1)
        recall = rec / col_len
        score = 2.0 * precision * recall / jnp.maximum(precision + recall, 0.5)
        x_ref[slot, h * HALF:(h + 1) * HALF, :] = score
        scores.append(score)
    x_ref[slot, 64:72, :] = jnp.broadcast_to(meta[4:5, :], (8, 128))
    t_ref[slot] = jnp.concatenate(scores + [id_ref[...]], axis=0).T[0:HALF, :]


def main_kernel(lens_ref, ids_ref, emb_ref, x_out, t_out,
                raw, turn, own_ref, len_ref, id_ref, meta_ref, vis, metas, best, row_best, x_mine, x_other, t_mine, t_got,
                raw_sem, send_sem, recv_sem, self_sem, meta_send, meta_recv, x_send, x_recv, t_send, t_recv):
    n_loop = lax.axis_size("loop")
    b, r = lax.axis_index("loop"), lax.axis_index("rep")
    other = 1 - r
    role = b % 4
    half, core = role // 2, role % 2
    early = 5 - 2 * half
    late = 8 - early
    partner = b + 1 - 2 * core

    def block(d):
        return (b + n_loop + d) % n_loop

    def by_role(values):
        v = values
        return v[0] * (1 - half) * (1 - core) + v[1] * (1 - half) * core + v[2] * half * (1 - core) + v[3] * half * core

    def copy(src, dst, ssem, rsem, blk, rp):
        return pltpu.make_async_remote_copy(src_ref=src, dst_ref=dst, send_sem=ssem, recv_sem=rsem,
                                            device_id={"loop": blk, "rep": rp}, device_id_type=MESH)

    def fetch(g):
        base = (r + (1 - 2 * r) * (g // 2)) * HALF + g % 2 * GROUP
        return pltpu.make_async_copy(emb_ref.at[pl.ds(base, GROUP)], raw.at[g], raw_sem.at[g])

    for g in range(4):
        fetch(g).start()
    barrier = pltpu.get_barrier_semaphore()
    peers = [(block(d), rp) for d in range(-BLOCK_REACH, BLOCK_REACH + 1) if d for rp in (r, other)]
    peers += [(b, other)]
    for blk, rp in peers:
        pl.semaphore_signal(barrier, inc=1, device_id={"loop": blk, "rep": rp}, device_id_type=MESH)
    turn[...] = turned_tokens()
    lane = lax.broadcasted_iota(jnp.int32, (1, 128), 1)
    even = lane // HALF % 2 == 0
    for ref, rows_ref, at in ((lens_ref, len_ref, 0), (ids_ref, id_ref, 4)):
        rows_ref[...] = rows_of(ref[...])
        line = ref[...].astype(jnp.float32)
        twice = jnp.concatenate([line, line], axis=1)
        rolled = pltpu.roll(twice, HALF, 1)
        meta_ref[0, at:at + 4, :] = jnp.broadcast_to(jnp.where(even, twice, rolled), (4, 128))
        meta_ref[1, at:at + 4, :] = jnp.broadcast_to(jnp.where(even, rolled, twice), (4, 128))
    metas[0] = meta_ref[r]

    def prepare_group(g, carry):
        h, q = r + (1 - 2 * r) * (g // 2), g % 2
        fetch(g).wait()

        def put(t, rows):
            own_ref[h, t // 4, t % 4, q] = rows

        lens = len_ref[pl.ds(pl.multiple_of(h * HALF + q * GROUP, GROUP), GROUP), :][:, 0:1]
        prepare(raw.at[g], turn[...], lens, put)
        return carry

    lax.fori_loop(0, 2, prepare_group, 0)

    def clear(i, carry):
        best[i // 2, i % 2] = jnp.full((ROWS, 128), -4.0, jnp.float32)
        return carry

    lax.fori_loop(0, 12, clear, 0)
    pl.semaphore_wait(barrier, len(peers))

    def move(kind, f, src, slot, blk, rp):
        return copy(src, vis.at[slot, f], send_sem.at[kind, f], recv_sem.at[slot, f], blk, rp)

    def arrived(slot, f):
        copy(vis.at[slot, f], vis.at[slot, f], send_sem.at[0, f], recv_sem.at[slot, f], partner, r).wait_recv()

    mine = own_ref.at[r]
    cross = own_ref.at[other]
    starts = {
        0: [(0, mine, 1, block(-4), r), (2, mine, 3, block(2), r)],
        1: [(0, mine, 1, block(-4), r), (4, mine, 5, block(-1), r), (5, mine, 0, block(4), r)],
        2: [(0, mine, 1, block(4), r)],
        3: [(0, mine, 1, block(4), r), (4, mine, 5, block(-1), r)],
    }
    crossing = {0: [], 1: [(2, cross, 3, block(2), other)], 2: [(4, cross, 5, block(-1), other)], 3: []}

    def first_moves(me, lists, then):
        def one(f, carry):
            for kind, src, slot, blk, rp in lists[me]:
                then(move(kind, f, src.at[f], slot, blk, rp))
            return carry

        if lists[me]:
            lax.fori_loop(0, PIECES, one, 0)

    for me in range(4):
        @pl.when(role == me)
        def _(me=me):
            first_moves(me, starts, lambda c: c.start())

    def meta_copy(k):
        blk = block(by_role([taken_offsets(me)[k] for me in range(4)]))
        return copy(meta_ref.at[r], metas.at[k + 1], meta_send.at[k], meta_recv.at[k], blk, r)

    for k in range(5):
        meta_copy(k).start()
    to_self = pltpu.make_async_copy(own_ref.at[r], vis.at[6], self_sem)
    to_self.start()
    lax.fori_loop(2, 4, prepare_group, 0)

    def after_early(f):
        return [(2, 7, vis.at[3, f], 5, block(1), r), (2, 3, vis.at[3, f], 0, block(-3), r)]

    def after_first(f):
        return [(0, 1, vis.at[1, f], 2, partner, r), (1, 1, vis.at[1, f], 2, partner, r),
                (2, 1, vis.at[1, f], 2, partner, r), (3, 1, vis.at[1, f], 2, partner, r),
                (2, 2, vis.at[1, f], 3, block(-2), r), (3, 2, vis.at[1, f], 3, block(-2), r)]

    def after_relay(f):
        return [(1, 6, vis.at[0, f], 4, block(1), r), (3, 6, vis.at[0, f], 4, block(-4), r)]

    def after_late(f):
        return [(0, 3, vis.at[3, f], 4, partner, r), (1, 3, vis.at[3, f], 4, partner, r)]

    def forward(list_of, f):
        for me in range(4):
            todo = [x for x in list_of(f) if x[0] == me]
            if todo:
                @pl.when(role == me)
                def _(todo=todo):
                    for _, kind, src, slot, blk, rp in todo:
                        move(kind, f, src, slot, blk, rp).start()

    def results(slot):
        out = [copy(x_mine.at[slot], x_other.at[slot], x_send.at[slot], x_recv.at[slot], b, other)]
        if slot:
            blk = block(by_role([OFFSETS[me][slot - 1] for me in range(4)]))
            for i, rp in enumerate((r, other)):
                out.append(copy(t_mine.at[slot], t_got.at[r, slot], t_send.at[i, slot], t_recv.at[r, slot], blk, rp))
        return out

    def send_results(slot):
        for c in results(slot):
            c.start()

    def send_either(one, two):
        pl.when(half == 0)(lambda: send_results(one))
        pl.when(half == 1)(lambda: send_results(two))

    def step(f, carry):
        odd = f % 2

        @pl.when(f < PIECES)
        def _():
            arrived(early, f)
            forward(after_early, f)
            arrived(1, f)
            forward(after_first, f)

            @pl.when(core == 1)
            def _():
                arrived(0, f)
                forward(after_relay, f)

        @pl.when(f > 0)
        def _():
            arrived(late, f - 1)
            forward(after_late, f - 1)

        @pl.when(f == PIECES - 1)
        def _():
            for k in range(5):
                copy(metas.at[k + 1], metas.at[k + 1], meta_send.at[k], meta_recv.at[k], partner, r).wait_recv()

        def part(i, carry):
            slot = odd * (early * (1 - i) + i) + (1 - odd) * ((1 - i) * (2 - i) + late * i * (2 - i) + 2 * i * (i - 1))
            n = (f - 1) // 2

            @pl.when((1 - odd) * (i - 1) != 0)
            def _():
                arrived(slot, 2 * n)
                arrived(slot, 2 * n + 1)

            @pl.when((f == PIECES) & (i == 0))
            def _():
                send_results(0)
                send_either(5, 3)
                send_results(1)

            @pl.when((f == PIECES) & (i == 1))
            def _():
                send_results(2)

            @pl.when((f == PIECES) & (i == 2))
            def _():
                send_either(3, 5)

            scored(slot, slot, n)
            return carry

        @pl.when(f > 0)
        def _():
            lax.fori_loop(0, 3 - odd, part, 0)
        return carry

    def scored(slot, source, n):
        cols = vis[source, pl.ds(2 * n, 2)].reshape(CHUNK, D)
        score_chunk(own_ref, cols, best, row_best, slot, n)

        @pl.when(n == CHUNKS - 1)
        def _():
            finish_scores(len_ref, id_ref, metas[slot], best, row_best, slot, x_mine, t_mine)

    for me in range(4):
        @pl.when(role == me)
        def _(me=me):
            first_moves(me, crossing, lambda c: c.start())

    to_self.wait()

    def self_step(n, carry):
        scored(0, 6, n)
        return carry

    lax.fori_loop(0, CHUNKS, self_step, 0)
    lax.fori_loop(0, PIECES + 1, step, 0)

    for slot in range(6):
        x_out[r, slot] = x_mine[slot]
    send_results(4)
    for slot in range(6):
        copy(x_mine.at[slot], x_other.at[slot], x_send.at[slot], x_recv.at[slot], b, other).wait_recv()
        x_out[other, slot] = x_other[slot]
    for slot in range(1, 6):
        for i in range(2):
            copy(t_mine.at[slot], t_got.at[i, slot], t_send.at[i, slot], t_recv.at[i, slot], b, other).wait_recv()
            t_out[i, slot - 1] = t_got[i, slot]

    for slot in range(6):
        for c in results(slot):
            c.wait_send()
    for k in range(5):
        meta_copy(k).wait_send()
    for me in range(4):
        @pl.when(role == me)
        def _(me=me):
            first_moves(me, starts, lambda c: c.wait_send())
            first_moves(me, crossing, lambda c: c.wait_send())

            def rest(f, carry):
                for list_of in (after_early, after_first, after_relay, after_late):
                    for who, kind, src, slot, blk, rp in list_of(f):
                        if who == me:
                            move(kind, f, src, slot, blk, rp).wait_send()
                return carry

            lax.fori_loop(0, PIECES, rest, 0)


def place_kernel(role_ref, ids_ref, x_ref, t_ref, table_ref, sum_ref):
    role = role_ref[0]
    lane = lax.broadcasted_iota(jnp.int32, (64, 128), 1)
    row = lax.broadcasted_iota(jnp.int32, (64, 128), 0)
    low = lane < 64
    first = (lane % 64) < 32
    ids = rows_of(ids_ref[...])

    def own(k):
        vals = jnp.where(first, x_ref[0, k, 0:64, :], x_ref[1, k, 0:64, :])
        theirs = jnp.where(first[0:8], x_ref[0, k, 64:72, :], x_ref[1, k, 64:72, :])
        return vals, jnp.concatenate([theirs] * 8, axis=0)

    def taken(k, upper):
        both = jnp.concatenate([t_ref[0, k], t_ref[1, k]], axis=0)
        turned = pltpu.roll(both, 64, 1)
        return (turned, both) if upper else (both, turned)

    for mine in range(4):
        @pl.when(role == mine)
        def _(mine=mine):
            taken_at = taken_offsets(mine)
            total = jnp.zeros((64, 128), jnp.float32)
            for p in range(6):
                parts = []
                for upper in range(2):
                    d = 2 * p + upper - BLOCK_REACH
                    if d > BLOCK_REACH:
                        parts.append(parts[0])
                        continue
                    if d == 0:
                        vals, theirs = own(0)
                        same = (theirs == ids) & ((lane % 64) != row)
                    else:
                        if d in OFFSETS[mine]:
                            vals, theirs = own(1 + OFFSETS[mine].index(d))
                        else:
                            vals, theirs = taken(taken_at.index(d), upper)
                        same = theirs == ids
                    inside = (lane >= 64) if upper else low
                    total = total + jnp.where(same & inside, vals, 0.0)
                    parts.append(vals)
                tile = jnp.where(low, parts[0], parts[1])
                width = 128 if p < 5 else 64
                table_ref[:, p * 128:p * 128 + width] = tile[:, 0:width]
            sums = jnp.sum(total, axis=1, keepdims=True)
            sum_ref[...] = jnp.broadcast_to(sums, (64, 128)).T[0:1, :]


def shards(embeddings, lengths, candidate_ids):
    lens, ids = lengths.reshape(1, -1), candidate_ids.reshape(1, -1)
    vmem, dma, f32 = pltpu.VMEM, pltpu.SemaphoreType.DMA, jnp.float32
    in_vmem = pl.BlockSpec(memory_space=pltpu.VMEM)
    x, t = pl.pallas_call(
        main_kernel,
        in_specs=[in_vmem, in_vmem, pl.BlockSpec(memory_space=pl.ANY)],
        out_specs=[in_vmem] * 2,
        out_shape=[jax.ShapeDtypeStruct((2, 6, 72, 128), f32), jax.ShapeDtypeStruct((2, 5, HALF, 128), f32)],
        scratch_shapes=[
            vmem((4, GROUP, TOK, D), jnp.bfloat16),
            vmem((256, 256), jnp.bfloat16),
            vmem((2, PIECES, 4, 2, GROUP, D), jnp.bfloat16),
            vmem((64, 128), f32),
            vmem((64, 128), f32),
            vmem((2, 8, 128), f32),
            vmem((7, PIECES, 4, 2, GROUP, D), jnp.bfloat16),
            vmem((6, 8, 128), f32),
            vmem((6, 2, ROWS, 128), f32),
            vmem((6, 2, CHUNKS, HALF, CHUNK), f32),
            vmem((6, 72, 128), f32),
            vmem((6, 72, 128), f32),
            vmem((6, HALF, 128), f32),
            vmem((2, 6, HALF, 128), f32),
            dma((4,)),
            dma((8, PIECES)),
            dma((6, PIECES)),
            dma,
            dma((5,)),
            dma((5,)),
            dma((6,)),
            dma((6,)),
            dma((2, 6)),
            dma((2, 6)),
        ],
        compiler_params=pltpu.CompilerParams(collective_id=0, has_side_effects=True, vmem_limit_bytes=56 << 20),
    )(lens, ids, embeddings)
    role = (lax.axis_index("loop") % 4).astype(jnp.int32).reshape(1)
    table, sums = pl.pallas_call(
        place_kernel,
        in_specs=[pl.BlockSpec(memory_space=pltpu.SMEM)] + [in_vmem] * 3,
        out_specs=[in_vmem] * 2,
        out_shape=[jax.ShapeDtypeStruct((64, 704), f32), jax.ShapeDtypeStruct((1, 64), f32)],
    )(role, ids, x, t)
    return table, sums.reshape(64)


def solution(mesh):
    placed = (P("loop", None, None), P("loop"), P("loop"))
    return jax.shard_map(
        shards, mesh=mesh, in_specs=placed, out_specs=(P("loop", None), P("loop")), check_vma=False
    )
```

```python
import jax
import jax.numpy as jnp
from jax import lax
from jax.experimental import pallas as pl
from jax.experimental.pallas import tpu as pltpu
from jax.sharding import PartitionSpec as P

BLOCK_REACH = 5
TOK = 32
HALF = 32
D = 1024
ROWS = TOK * HALF
GROUP = 16
PIECES = 16
MESH = pl.DeviceIdType.MESH
OFFSETS = ((4, 5, -2, -1, 1), (4, 3, -2, -3, 1), (-4, -3, -2, -5, 1), (-4, -5, -2, 5, -3))


def taken_offsets(role):
    found = []
    for k in range(5):
        for other in range(4):
            if (other + OFFSETS[other][k]) % 4 == role:
                found.append(-OFFSETS[other][k])
    return found


def rows_of(line):
    return jnp.broadcast_to(line.astype(jnp.float32), (128, 64)).T


def turned_tokens():
    out = lax.broadcasted_iota(jnp.int32, (256, 256), 0)
    into = lax.broadcasted_iota(jnp.int32, (256, 256), 1)
    hit = (out // 16 == into % 16) & (out % 16 == into // 16)
    return jnp.where(hit, 1.0, 0.0).astype(jnp.bfloat16)


def prepare(emb, turn, lens, put):
    first = None
    for g in range(TOK // 16):
        raw = emb[:, g * 16:(g + 1) * 16, :].reshape(256, D)
        x = jnp.dot(turn, raw, preferred_element_type=jnp.float32)
        for t in range(16):
            rows = x[t * GROUP:(t + 1) * GROUP, :]
            ms = jnp.sum(rows * rows, axis=1, keepdims=True) * (1.0 / D)
            rows = rows * (lax.rsqrt(ms + 1e-06) * (1.0 / 32.0))
            if first is None:
                first = rows
            else:
                rows = jnp.where(lens > float(g * 16 + t), rows, first)
            put(g * 16 + t, rows.astype(jnp.bfloat16))


def score_piece(own_ref, cols, best_ref, row_best_ref, acc, e):
    for h in range(2):
        s = lax.dot_general(own_ref[h].reshape(ROWS, D), cols,
                            (((1,), (1,)), ((), ())), preferred_element_type=jnp.float32)
        row_best_ref[acc, h, e] = jnp.max(s.reshape(TOK, HALF, 256), axis=0)
        best_ref[acc, h] = jnp.maximum(best_ref[acc, h], jnp.maximum(s[:, 0:128], s[:, 128:256]))


def finish_scores(len_ref, id_ref, col_len, col_id, best_ref, row_best_ref, acc, x_ref, t_ref):
    twice = acc == 0
    lane = lax.broadcasted_iota(jnp.int32, (1, 128), 1)
    scores = []
    for h in range(2):
        row_len = len_ref[h * HALF:(h + 1) * HALF, :]

        def add(t, total):
            b = best_ref[acc, h, pl.ds(pl.multiple_of(t * HALF, HALF), HALF), :]
            if twice:
                b = jnp.maximum(b, pltpu.roll(b, 64, 1))
            return total + jnp.where(row_len > t.astype(jnp.float32), b, 0.0)

        def add_rows(e, total):
            for k in range(2):
                u = (2 * e + k).astype(jnp.float32)
                if twice:
                    u = u + jnp.where(lane < 64, 0.0, 16.0)
                total = total + jnp.where(u < col_len, row_best_ref[acc, h, e, :, k * 128:(k + 1) * 128], 0.0)
            return total

        zero = jnp.zeros((HALF, 128), jnp.float32)
        precision = lax.fori_loop(0, TOK, add, zero, unroll=8) / row_len
        rec = lax.fori_loop(0, PIECES // 2 if twice else PIECES, add_rows, zero, unroll=4)
        if twice:
            rec = rec + pltpu.roll(rec, 64, 1)
        recall = rec / col_len
        score = 2.0 * precision * recall / jnp.maximum(precision + recall, 0.5)
        x_ref[acc, h * HALF:(h + 1) * HALF, :] = score
        scores.append(score)
    x_ref[acc, 64:72, :] = jnp.broadcast_to(col_id, (8, 128))
    t_ref[acc] = jnp.concatenate(scores + [id_ref[...]], axis=0).T


def main_kernel(lens_ref, ids_ref, emb_ref, x_out, t_out,
                raw, turn, own_ref, len_ref, id_ref, meta_ref, vis, metas, best, row_best, x_mine, x_other, t_mine, t_got,
                raw_sem, send_sem, recv_sem, self_sem, meta_send, meta_recv, x_send, x_recv, t_send, t_recv):
    n_loop = lax.axis_size("loop")
    b, r = lax.axis_index("loop"), lax.axis_index("rep")
    other = 1 - r
    role = b % 4
    half, core = role // 2, role % 2
    early = 5 - 2 * half * core
    late = 8 - early
    partner = b + 1 - 2 * core

    def block(d):
        return (b + n_loop + d) % n_loop

    def by_role(values):
        v = values
        return v[0] * (1 - half) * (1 - core) + v[1] * (1 - half) * core + v[2] * half * (1 - core) + v[3] * half * core

    def copy(src, dst, ssem, rsem, blk, rp):
        return pltpu.make_async_remote_copy(src_ref=src, dst_ref=dst, send_sem=ssem, recv_sem=rsem,
                                            device_id={"loop": blk, "rep": rp}, device_id_type=MESH)

    def fetch(g):
        base = (r + (1 - 2 * r) * (g // 2)) * HALF + g % 2 * GROUP
        return pltpu.make_async_copy(emb_ref.at[pl.ds(base, GROUP)], raw.at[g], raw_sem.at[g])

    for g in range(4):
        fetch(g).start()
    barrier = pltpu.get_barrier_semaphore()
    peers = [(block(d), rp) for d in range(-BLOCK_REACH, BLOCK_REACH + 1) if d for rp in (r, other)]
    peers += [(b, other)]
    for blk, rp in peers:
        pl.semaphore_signal(barrier, inc=1, device_id={"loop": blk, "rep": rp}, device_id_type=MESH)
    turn[...] = turned_tokens()
    lane = lax.broadcasted_iota(jnp.int32, (1, 128), 1)
    even = lane // HALF % 2 == 0
    for ref, rows_ref, at in ((lens_ref, len_ref, 0), (ids_ref, id_ref, 4)):
        rows_ref[...] = rows_of(ref[...])
        line = ref[...].astype(jnp.float32)
        twice = jnp.concatenate([line, line], axis=1)
        rolled = pltpu.roll(twice, HALF, 1)
        meta_ref[0, at:at + 4, :] = jnp.broadcast_to(jnp.where(even, twice, rolled), (4, 128))
        meta_ref[1, at:at + 4, :] = jnp.broadcast_to(jnp.where(even, rolled, twice), (4, 128))
    metas[0] = meta_ref[r]

    def prepare_group(g, carry):
        h, q = r + (1 - 2 * r) * (g // 2), g % 2
        fetch(g).wait()

        def put(t, rows):
            own_ref[h, t // 2, t % 2, q] = rows

        lens = len_ref[pl.ds(pl.multiple_of(h * HALF + q * GROUP, GROUP), GROUP), :][:, 0:1]
        prepare(raw.at[g], turn[...], lens, put)
        return carry

    lax.fori_loop(0, 2, prepare_group, 0)

    def clear(i, carry):
        best[i // 2, i % 2] = jnp.full((ROWS, 128), -4.0, jnp.float32)
        return carry

    lax.fori_loop(0, 4, clear, 0)
    pl.semaphore_wait(barrier, len(peers))

    def move(kind, f, src, slot, blk, rp):
        return copy(src, vis.at[slot, f], send_sem.at[kind, f], recv_sem.at[slot, f], blk, rp)

    def arrived(slot, f):
        copy(vis.at[slot, f], vis.at[slot, f], send_sem.at[0, f], recv_sem.at[slot, f], partner, r).wait_recv()

    mine = own_ref.at[r]
    cross = own_ref.at[other]
    starts = {
        0: [(0, mine, 1, block(-4), r), (2, mine, 3, block(2), r)],
        1: [(0, mine, 1, block(-4), r), (4, mine, 5, block(-1), r)],
        2: [(0, mine, 1, block(4), r)],
        3: [(0, mine, 1, block(4), r), (4, mine, 5, block(-1), r)],
    }
    crossing = {0: [], 1: [(2, cross, 3, block(2), other)], 2: [(4, cross, 5, block(-1), other)], 3: []}

    def first_moves(me, lists, then):
        def one(f, carry):
            for kind, src, slot, blk, rp in lists[me]:
                then(move(kind, f, src.at[f], slot, blk, rp))
            return carry

        if lists[me]:
            lax.fori_loop(0, PIECES, one, 0)

    for me in range(4):
        @pl.when(role == me)
        def _(me=me):
            first_moves(me, starts, lambda c: c.start())

    def meta_copy(k):
        blk = block(by_role([taken_offsets(me)[k] for me in range(4)]))
        return copy(meta_ref.at[r], metas.at[k + 1], meta_send.at[k], meta_recv.at[k], blk, r)

    for k in range(5):
        meta_copy(k).start()
    to_self = pltpu.make_async_copy(own_ref.at[r], vis.at[6], self_sem)
    to_self.start()
    lax.fori_loop(2, 4, prepare_group, 0)

    def after_first(f):
        return [(0, 1, vis.at[1, f], 2, partner, r), (1, 1, vis.at[1, f], 2, partner, r),
                (2, 1, vis.at[1, f], 2, partner, r), (3, 1, vis.at[1, f], 2, partner, r),
                (2, 2, vis.at[1, f], 3, block(-2), r), (3, 2, vis.at[1, f], 3, block(-2), r)]

    def after_third(f):
        return [(0, 3, vis.at[3, f], 4, partner, r), (1, 3, vis.at[3, f], 4, partner, r),
                (2, 7, vis.at[3, f], 5, block(1), r), (2, 3, vis.at[3, f], 0, block(-3), r)]

    def after_relay(f):
        return [(3, 6, vis.at[0, f], 4, block(-4), r)]

    def ahead(f):
        return [(1, 5, mine.at[f], 4, block(5), r)]

    def forward(list_of, f, only=range(4)):
        for me in only:
            todo = [x for x in list_of(f) if x[0] == me]
            if todo:
                @pl.when(role == me)
                def _(todo=todo):
                    for _, kind, src, slot, blk, rp in todo:
                        move(kind, f, src, slot, blk, rp).start()

    def x_copy(acc):
        return copy(x_mine.at[acc], x_other.at[acc], x_send.at[acc], x_recv.at[acc], b, other)

    def t_copies(acc, v):
        if acc == 0:
            slot, picked = early, [2 if me == 3 else 4 for me in range(4)]
        elif v == 2:
            slot, picked = late, [4 if me == 3 else 2 for me in range(4)]
        else:
            slot, picked = (1, 2, None, 4)[v], [(0, 1, None, 3)[v]] * 4
        blk = block(by_role([OFFSETS[me][picked[me]] for me in range(4)]))
        src = t_mine.at[acc, pl.ds(v * HALF, HALF)]
        sem = 4 if acc == 0 else v
        return [copy(src, t_got.at[r, slot - 1], t_send.at[i, sem], t_recv.at[r, slot - 1], blk, rp)
                for i, rp in enumerate((r, other))]

    def results(acc):
        out = [x_copy(acc)]
        for v in ((1,) if acc == 0 else range(4)):
            out += t_copies(acc, v)
        return out

    group = lax.broadcasted_iota(jnp.int32, (1, 128), 1) // HALF

    def finish(acc):
        def lanes(at):
            row = lambda k: metas[k, at:at + 1, :]
            if acc == 0:
                return jnp.where(group % 2 == 0, row(0), row(early))
            return jnp.where(group < 2, jnp.where(group == 0, row(1), row(2)), jnp.where(group == 2, row(late), row(4)))

        finish_scores(len_ref, id_ref, lanes(0), lanes(4), best, row_best, acc, x_mine, t_mine)

    def step(f, carry):
        @pl.when(f < PIECES)
        def _():
            arrived(1, f)
            forward(after_first, f)

            @pl.when(role == 2)
            def _():
                arrived(3, f)
                forward(after_third, f, (2,))

        @pl.when((f > 0) & (f <= PIECES))
        def _():
            @pl.when(half == 0)
            def _():
                arrived(3, f - 1)
                forward(after_third, f - 1, (0, 1))

            @pl.when(role == 3)
            def _():
                arrived(0, f - 1)
                forward(after_relay, f - 1)

        @pl.when((f >= 3) & (f < 13))
        def _():
            forward(ahead, f - 3)

        @pl.when((f >= 13) & (f < PIECES))
        def _():
            forward(ahead, 2 * f - 16)
            forward(ahead, 2 * f - 15)

        def part(i, carry):
            e = f - 4 + i
            far = e + 8 * (1 - i)

            @pl.when(i == 0)
            def _():
                arrived(early, e)
                arrived(early, far)

            @pl.when(i == 1)
            def _():
                arrived(2, e)
                arrived(4, e)
                pl.when(role == 3)(lambda: arrived(5, e))

            slots = (6 - 5 * i, early * (1 - i) + 2 * i, 6 * (1 - i) + late * i, early * (1 - i) + 4 * i)
            places = (e, e, far, far)
            cols = jnp.concatenate([vis[slot, at, k].reshape(HALF, D) for k in range(2)
                                    for slot, at in zip(slots, places)], axis=0)
            score_piece(own_ref, cols, best, row_best, i, e)
            return carry

        window = (f + 4) // 8
        lax.fori_loop(1 - window * (2 - window), 1 + (f + 13) // 16, part, 0)

        @pl.when(f == 12)
        def _():
            for k in range(5):
                copy(metas.at[k + 1], metas.at[k + 1], meta_send.at[k], meta_recv.at[k], partner, r).wait_recv()
            finish(0)

        @pl.when(f == 13)
        def _():
            for c in results(0):
                c.start()
        return carry

    for me in range(4):
        @pl.when(role == me)
        def _(me=me):
            first_moves(me, crossing, lambda c: c.start())

    to_self.wait()
    lax.fori_loop(0, PIECES + 3, step, 0)
    finish(1)
    for acc in range(2):
        x_out[r, acc] = x_mine[acc]
    for c in results(1):
        c.start()
    for acc in range(2):
        x_copy(acc).wait_recv()
        x_out[other, acc] = x_other[acc]
    for k in range(5):
        for i in range(2):
            copy(t_got.at[i, k], t_got.at[i, k], t_send.at[i, k], t_recv.at[i, k], b, other).wait_recv()
            t_out[i, k] = t_got[i, k]

    for acc in range(2):
        for c in results(acc):
            c.wait_send()
    for k in range(5):
        meta_copy(k).wait_send()
    for me in range(4):
        @pl.when(role == me)
        def _(me=me):
            first_moves(me, starts, lambda c: c.wait_send())
            first_moves(me, crossing, lambda c: c.wait_send())

            def rest(f, carry):
                for list_of in (after_first, after_third, after_relay, ahead):
                    for who, kind, src, slot, blk, rp in list_of(f):
                        if who == me:
                            move(kind, f, src, slot, blk, rp).wait_send()
                return carry

            lax.fori_loop(0, PIECES, rest, 0)


def place_kernel(role_ref, ids_ref, x_ref, t_ref, table_ref, sum_ref):
    role = role_ref[0]
    lane = lax.broadcasted_iota(jnp.int32, (64, 128), 1)
    row = lax.broadcasted_iota(jnp.int32, (64, 128), 0)
    low = lane < 64
    first = (lane % 64) < 32
    ids = rows_of(ids_ref[...])

    def own(acc, v, upper):
        turned = [pltpu.roll(x_ref[c, acc], (upper * 64 + (c - v) * HALF) % 128, 1) for c in range(2)]
        both = jnp.where(first, turned[0][0:64, :], turned[1][0:64, :])
        theirs = jnp.where(first[0:8], turned[0][64:72, :], turned[1][64:72, :])
        return both, jnp.concatenate([theirs] * 8, axis=0)

    def taken(k, upper):
        both = jnp.concatenate([t_ref[0, k], t_ref[1, k]], axis=0)
        turned = pltpu.roll(both, 64, 1)
        return (turned, both) if upper else (both, turned)

    for mine in range(4):
        @pl.when(role == mine)
        def _(mine=mine):
            taken_at = taken_offsets(mine)
            total = jnp.zeros((64, 128), jnp.float32)
            for p in range(6):
                parts = []
                for upper in range(2):
                    d = 2 * p + upper - BLOCK_REACH
                    if d > BLOCK_REACH:
                        parts.append(parts[0])
                        continue
                    if d == 0:
                        vals, theirs = own(0, 0, upper)
                        same = (theirs == ids) & ((lane % 64) != row)
                    else:
                        if d in OFFSETS[mine]:
                            k = 1 + OFFSETS[mine].index(d)
                            spot = (0, 1) if k == (3 if mine == 3 else 5) else (1, 2 if k in (3, 5) else (None, 0, 1, None, 3)[k])
                            vals, theirs = own(*spot, upper)
                        else:
                            vals, theirs = taken(taken_at.index(d), upper)
                        same = theirs == ids
                    inside = (lane >= 64) if upper else low
                    total = total + jnp.where(same & inside, vals, 0.0)
                    parts.append(vals)
                tile = jnp.where(low, parts[0], parts[1])
                width = 128 if p < 5 else 64
                table_ref[:, p * 128:p * 128 + width] = tile[:, 0:width]
            sums = jnp.sum(total, axis=1, keepdims=True)
            sum_ref[...] = jnp.broadcast_to(sums, (64, 128)).T[0:1, :]


def shards(embeddings, lengths, candidate_ids):
    lens, ids = lengths.reshape(1, -1), candidate_ids.reshape(1, -1)
    vmem, dma, f32 = pltpu.VMEM, pltpu.SemaphoreType.DMA, jnp.float32
    in_vmem = pl.BlockSpec(memory_space=pltpu.VMEM)
    x, t = pl.pallas_call(
        main_kernel,
        in_specs=[in_vmem, in_vmem, pl.BlockSpec(memory_space=pl.ANY)],
        out_specs=[in_vmem] * 2,
        out_shape=[jax.ShapeDtypeStruct((2, 2, 72, 128), f32), jax.ShapeDtypeStruct((2, 5, HALF, 128), f32)],
        scratch_shapes=[
            vmem((4, GROUP, TOK, D), jnp.bfloat16),
            vmem((256, 256), jnp.bfloat16),
            vmem((2, PIECES, 2, 2, GROUP, D), jnp.bfloat16),
            vmem((64, 128), f32),
            vmem((64, 128), f32),
            vmem((2, 8, 128), f32),
            vmem((7, PIECES, 2, 2, GROUP, D), jnp.bfloat16),
            vmem((6, 8, 128), f32),
            vmem((2, 2, ROWS, 128), f32),
            vmem((2, 2, PIECES, HALF, 256), f32),
            vmem((2, 72, 128), f32),
            vmem((2, 72, 128), f32),
            vmem((2, 128, 128), f32),
            vmem((2, 5, HALF, 128), f32),
            dma((4,)),
            dma((8, PIECES)),
            dma((6, PIECES)),
            dma,
            dma((5,)),
            dma((5,)),
            dma((2,)),
            dma((2,)),
            dma((2, 5)),
            dma((2, 5)),
        ],
        compiler_params=pltpu.CompilerParams(collective_id=0, has_side_effects=True, vmem_limit_bytes=56 << 20),
    )(lens, ids, embeddings)
    role = (lax.axis_index("loop") % 4).astype(jnp.int32).reshape(1)
    table, sums = pl.pallas_call(
        place_kernel,
        in_specs=[pl.BlockSpec(memory_space=pltpu.SMEM)] + [in_vmem] * 3,
        out_specs=[in_vmem] * 2,
        out_shape=[jax.ShapeDtypeStruct((64, 704), f32), jax.ShapeDtypeStruct((1, 64), f32)],
    )(role, ids, x, t)
    return table, sums.reshape(64)


def solution(mesh):
    placed = (P("loop", None, None), P("loop"), P("loop"))
    return jax.shard_map(
        shards, mesh=mesh, in_specs=placed, out_specs=(P("loop", None), P("loop")), check_vma=False
    )
```
